512 devices in a mesh: doc: 16 (over y_hi, z), ctx: 32 (over x, y_lo, core).
Axes of the slice: x: 4, y: 8 (y_hi: 2, y_lo: 4; y = y_hi * 4 + y_lo), z: 8, core: 2. Of those that a mesh axis runs over, the one named last changes fastest.
Arguments:
- queries: bfloat16 [16, 4096, 4096], P('doc', 'ctx'), may hold values from -6 to 6
- out_grad: bfloat16 [16, 4096, 4096], P('doc', 'ctx'), may hold values from -6 to 6
- mem_keys: bfloat16 [16, 64, 4096], P('doc', 'ctx'), may hold values from -6 to 6
- mem_values: bfloat16 [16, 64, 4096], P('doc', 'ctx'), may hold values from -6 to 6
Outputs:
- grad_queries: float32 [16, 4096, 4096], P('doc', 'ctx')
- grad_keys: float32 [16, 64, 4096], P('doc', 'ctx')
- grad_values: float32 [16, 64, 4096], P('doc', 'ctx')
The draws below stay inside these ranges and needn't reach their ends.
All inputs are finite; a program needn't handle non-finite values.
Results may differ from the reference program's by a relative error of at most 0.0011.
Values may be sent and summed in bfloat16 or wider, within the bound.
No kernel may reach another device: no remote copies, remote signals or barrier semaphores. Data moves between devices by JAX's collectives and lax.ppermute only.
A program may use at most 64 MiB of HBM per device.

```python
import math
import jax
import jax.numpy as jnp
from jax import lax

HEADS = 32
HD = 128
MEM = 64
QLEN = 4096
DOCS = 16


def draw_mem_keys(key, part):
    first, second = jax.random.split(key, 2)
    row_scale = jnp.exp(jax.random.uniform(second, (DOCS, MEM, HEADS, 1), jnp.float32, math.log(0.25), math.log(2.5)))
    doc_scale = 0.7 + 0.6 * jnp.arange(DOCS, dtype=jnp.float32) / max(DOCS - 1, 1)
    doc_scale = doc_scale.reshape(DOCS, 1, 1, 1)
    base = jax.random.truncated_normal(first, -4.0, 4.0, (DOCS, MEM, HEADS, HD), jnp.float32)
    return (0.4 * base * row_scale * doc_scale).reshape(DOCS, MEM, HEADS * HD).astype(jnp.bfloat16)


def block_scale(rng, extent, cuts, low, top_value):
    gain = 1.0
    for position, parts in cuts:
        heights = jax.random.uniform(jax.random.fold_in(jax.random.fold_in(rng, 6), position), (parts,), jnp.float32, low / len(cuts), top_value / len(cuts))
        gain = gain * jnp.repeat(jnp.exp(heights), extent[position] // parts).reshape((-1,) + (1,) * (len(extent) - 1 - position))
    return gain


def bell_draw(own_key, shape, width, most, shards=(), kind=jnp.bfloat16):
    loudness = block_scale(own_key, shape, shards, -0.22, 0.18) if shards else 1.0
    values = jax.random.normal(own_key, shape, jnp.float32) * width * loudness
    return jnp.minimum(jnp.maximum(values, -most), most).astype(kind)


def setup_inputs(seed: int = 0) -> dict:
    keys = jax.random.split(jax.random.key(seed), 5)
    queries = bell_draw(keys[0], (DOCS, QLEN, HEADS * HD), 1.0, 6.0, ((0, 16), (1, 32)))
    out_grad = bell_draw(keys[1], (DOCS, QLEN, HEADS * HD), 1.0, 6.0, ((0, 16), (1, 32)))
    mem_keys = draw_mem_keys(jax.random.fold_in(keys[4], 71), 0)
    mem_values = bell_draw(keys[3], (DOCS, MEM, HEADS * HD), 1.0, 6.0, ((0, 16), (1, 32)))
    return dict(queries=queries, out_grad=out_grad, mem_keys=mem_keys, mem_values=mem_values)


def reference(queries, out_grad, mem_keys, mem_values):
    scale = HD ** -0.5
    high = lax.Precision.HIGHEST

    def split(x):
        return jnp.transpose(x.astype(jnp.float32).reshape(-1, HEADS, HD), (1, 0, 2))

    def one_head(items):
        q_rows, g_rows, k_rows, v_rows = items
        expo = jnp.exp(jnp.dot(q_rows, k_rows.T, precision=high) * scale)
        dprob = jnp.dot(g_rows, v_rows.T, precision=high)
        norm = jnp.sum(expo, axis=1, keepdims=True)
        drift = jnp.sum(expo * dprob, axis=1, keepdims=True) / norm
        prob = expo / norm
        dscore = prob * (dprob - drift)
        grad_q = jnp.dot(dscore, k_rows, precision=high) * scale
        grad_k = jnp.dot(dscore.T, q_rows, precision=high) * scale
        grad_v = jnp.dot(prob.T, g_rows, precision=high)
        return grad_q, grad_k, grad_v

    grad_q, grad_k, grad_v = lax.map(one_head, (split(queries), split(out_grad), split(mem_keys), split(mem_values)))

    def join(x, rows):
        return jnp.transpose(x, (1, 0, 2)).reshape(DOCS, rows, HEADS * HD)

    return join(grad_q, QLEN), join(grad_k, MEM), join(grad_v, MEM)
```

```python
import jax
import jax.numpy as jnp
from jax import lax
from jax.experimental import pallas as pl
from jax.experimental.pallas import tpu as pltpu
from jax.sharding import PartitionSpec as P


HD = 128
SCALE = HD ** (-0.5)
CHUNKS = (96, 32)
QBLOCK = 512
TILE = 8
HALF_BITS = 14.0
F32 = jnp.float32
BF16 = jnp.bfloat16
HALF = jnp.float16


def dot(a, b, da, db):
    return lax.dot_general(a, b, (((da,), (db,)), ((), ())), preferred_element_type=F32)


def split(x):
    hi = x.astype(BF16)
    return hi, (x - hi.astype(F32)).astype(BF16)


def exponent(top):
    return jnp.ceil(jnp.log2(jnp.maximum(top, 1e-30))) - HALF_BITS


def by_head(queries, out_grad, mem_keys, mem_values, chunks):
    rows, width = queries.shape
    mem = mem_keys.shape[0]
    nheads = width // HD
    group = min(nheads, 8)

    def kernel(q_ref, g_ref, k_ref, v_ref, *outs):
        k = k_ref[...].astype(F32)
        v = v_ref[...].astype(F32)
        fill = jnp.zeros((TILE - 2 * mem, HD), F32)
        for h in range(group):
            cols = slice(h * HD, (h + 1) * HD)
            start = 0
            for out, part in zip(outs, chunks):
                out[h, :part, :] = q_ref[start:start + part, cols]
                out[h, part:2 * part, :] = g_ref[start:start + part, cols]
                start += part
            outs[0][h, 2 * chunks[0]:, :] = jnp.concatenate([k[:, cols], v[:, cols], fill], axis=0).astype(BF16)

    sizes = [2 * part + (TILE if c == 0 else 0) for c, part in enumerate(chunks)]
    return pl.pallas_call(
        kernel,
        grid=(nheads // group,),
        in_specs=[pl.BlockSpec((rows, group * HD), lambda i: (0, i))] * 2
        + [pl.BlockSpec((mem, group * HD), lambda i: (0, i))] * 2,
        out_specs=[pl.BlockSpec((group, size, HD), lambda i: (i, 0, 0)) for size in sizes],
        out_shape=[jax.ShapeDtypeStruct((nheads, size, HD), BF16) for size in sizes],
        cost_estimate=pl.CostEstimate(flops=0, bytes_accessed=8 * rows * width, transcendentals=0),
        name="by_head",
    )(queries, out_grad, mem_keys, mem_values)


def memory_copies(block, part, rows, ndoc):
    ndev = block.shape[0]
    total = ndev * rows

    def kernel(x_ref, out, tmp):
        x = x_ref[...].astype(F32)
        for c in range(ndev):
            tmp[c * rows:(c + 1) * rows, :] = x[c, :rows, :]
            tmp[total + c * rows:total + (c + 1) * rows, :] = x[c, rows:2 * rows, :]
        whole = tmp[...].astype(BF16)
        for d in range(ndoc):
            out[d] = whole

    return pl.pallas_call(
        kernel,
        grid=(1,),
        in_specs=[pl.BlockSpec((ndev, TILE, HD), lambda i: (0, 2 * part // TILE, 0))],
        out_specs=pl.BlockSpec((ndoc, 2 * total, HD), lambda i: (0, 0, 0)),
        out_shape=jax.ShapeDtypeStruct((ndoc, 2 * total, HD), BF16),
        scratch_shapes=[pltpu.VMEM((2 * total, HD), F32)],
        cost_estimate=pl.CostEstimate(flops=0, bytes_accessed=4 * ndoc * total * HD, transcendentals=0),
        compiler_params=pltpu.CompilerParams(vmem_limit_bytes=4 << 20),
        name="memory_copies",
    )(block)


def attention_grads(rows, part, memory, before, last):
    ndev = rows.shape[0]
    ndoc, both_mem, _ = memory.shape
    mem = both_mem // 2
    total = ndoc * mem
    per = max(1, min(ndev, QBLOCK // part))
    while ndev % per:
        per -= 1
    block = per * part
    steps = ndev // per
    size = both_mem + (TILE if last else 0)

    def kernel(*refs):
        if before is None:
            x_ref, m_ref, gq_ref, power_ref, sums_ref, k_ref, v_ref, top_ref = refs
        else:
            x_ref, m_ref, before_ref, gq_ref, power_ref, sums_ref, k_ref, v_ref, top_ref = refs
        acc_ref = sums_ref.at[:, :both_mem, :]
        step = pl.program_id(0)

        @pl.when(step == 0)
        def _():
            acc_ref[...] = jnp.zeros_like(acc_ref) if before is None else before_ref[...]
            k_ref[...] = m_ref[:, :mem, :].reshape(total, HD)
            v_ref[...] = m_ref[:, mem:, :].reshape(total, HD)
            top_ref[...] = jnp.zeros_like(top_ref)

        q = x_ref[:, :part, :].reshape(block, HD)
        g = x_ref[:, part:2 * part, :].reshape(block, HD)
        k = k_ref[...]
        v = v_ref[...]
        expo = jnp.exp(dot(k, q, 1, 1) * SCALE)
        dprob = dot(v, g, 1, 1)
        norm = jnp.sum(expo, axis=0, keepdims=True)
        drift = jnp.sum(expo * dprob, axis=0, keepdims=True) / norm
        prob = expo * (1.0 / norm)
        dscore = prob * (dprob - drift)
        p_hi, p_lo = split(prob)
        s_hi, s_lo = split(dscore)
        grad_v = dot(p_hi, g, 1, 0) + dot(p_lo, g, 1, 0)
        grad_k = (dot(s_hi, q, 1, 0) + dot(s_lo, q, 1, 0)) * SCALE
        grad_q = (dot(s_hi, k, 0, 0) + dot(s_lo, k, 0, 0)) * SCALE
        gq_ref[pl.ds(pl.multiple_of(step * block, block), block), :] = grad_q
        top_ref[...] = jnp.maximum(top_ref[...], jnp.max(jnp.abs(grad_q), axis=0, keepdims=True))
        acc_ref[:, :mem, :] += grad_k.reshape(ndoc, mem, HD)
        acc_ref[:, mem:, :] += grad_v.reshape(ndoc, mem, HD)

        @pl.when(step == steps - 1)
        def _():
            power = exponent(jnp.max(top_ref[...], axis=1, keepdims=True))
            gq_ref[...] = gq_ref[...] * jnp.exp2(-power)
            power_ref[...] = jnp.broadcast_to(power, power_ref.shape)
            if last:
                first = lax.broadcasted_iota(jnp.int32, (TILE, HD), 0) == 0
                powers = []
                for start in (0, mem):
                    x = acc_ref[:, start:start + mem, :]
                    top = jnp.max(jnp.max(jnp.max(jnp.abs(x), axis=0), axis=0, keepdims=True), axis=1, keepdims=True)
                    power = exponent(top)
                    acc_ref[:, start:start + mem, :] = x * jnp.exp2(-power).reshape(1, 1, 1)
                    powers.append(jnp.broadcast_to(power, (TILE, HD)))
                tail = jnp.where(first, powers[0], powers[1])
                for d in range(ndoc):
                    sums_ref[d, both_mem:, :] = tail

    def whole(*shape):
        return pl.BlockSpec(shape, lambda i: (0,) * len(shape))

    args = (rows, memory) if before is None else (rows, memory, before)
    return pl.pallas_call(
        kernel,
        grid=(steps,),
        in_specs=[pl.BlockSpec((per, 2 * part, HD), lambda i: (i, 0, 0))]
        + [whole(ndoc, both_mem, HD)] * (len(args) - 1),
        out_specs=[whole(ndev * part, HD), whole(1, HD), whole(ndoc, size, HD)],
        out_shape=[
            jax.ShapeDtypeStruct((ndev * part, HD), F32),
            jax.ShapeDtypeStruct((1, HD), F32),
            jax.ShapeDtypeStruct((ndoc, size, HD), F32),
        ],
        scratch_shapes=[pltpu.VMEM((total, HD), BF16)] * 2 + [pltpu.VMEM((1, HD), F32)],
        cost_estimate=pl.CostEstimate(
            flops=16 * ndev * part * total * HD,
            bytes_accessed=8 * ndev * part * HD,
            transcendentals=ndev * part * total,
        ),
        compiler_params=pltpu.CompilerParams(vmem_limit_bytes=24 << 20),
        name="attention_grads",
    )(*args)


def memory_sums(parts, powers, ndev):
    ndoc = parts.shape[0]
    mem = (parts.shape[1] - TILE) // 2
    rows = mem // ndev

    def kernel(x_ref, *refs):
        out = refs[-1]
        terms = []
        last = [p[...] for p in refs[:-1]]
        for v in (0, 1):
            total = jnp.zeros((mem, HD), F32)
            for d in range(ndoc):
                total = total + x_ref[d, v * mem:(v + 1) * mem, :] * jnp.exp2(x_ref[d, 2 * mem + v:2 * mem + v + 1, :])
            top = jnp.max(jnp.max(jnp.abs(total), axis=0, keepdims=True), axis=1, keepdims=True)
            power = exponent(top)
            total = total * jnp.exp2(-power)
            high = total.astype(BF16).astype(F32)
            terms += [high, total - high]
            last.append(jnp.broadcast_to(power, (1, HD)))
        last = jnp.concatenate(last + [jnp.zeros((2 * TILE - 4 * rows - len(last), HD), F32)], axis=0)
        for c in range(ndev):
            for t, term in enumerate(terms):
                out[c, t * rows:(t + 1) * rows, :] = term[c * rows:(c + 1) * rows, :]
            out[c, 4 * rows:, :] = last

    return pl.pallas_call(
        kernel,
        out_shape=jax.ShapeDtypeStruct((ndev, 2 * TILE, HD), F32),
        cost_estimate=pl.CostEstimate(flops=0, bytes_accessed=4 * parts.size, transcendentals=0),
        compiler_params=pltpu.CompilerParams(vmem_limit_bytes=6 << 20),
        name="memory_sums",
    )(parts, *powers)


def memory_rows(tail, rows, at):
    nheads = tail.shape[0]

    def kernel(x_ref, k_ref, v_ref):
        for h in range(nheads):
            cols = slice(h * HD, (h + 1) * HD)
            scale = jnp.exp2(x_ref[h, at:at + 2, :])
            k_ref[:, cols] = (x_ref[h, :rows, :] + x_ref[h, rows:2 * rows, :]) * scale[:1]
            v_ref[:, cols] = (x_ref[h, 2 * rows:3 * rows, :] + x_ref[h, 3 * rows:4 * rows, :]) * scale[1:]

    return pl.pallas_call(
        kernel,
        out_shape=[jax.ShapeDtypeStruct((rows, nheads * HD), F32)] * 2,
        cost_estimate=pl.CostEstimate(flops=0, bytes_accessed=16 * nheads * TILE * HD, transcendentals=0),
        compiler_params=pltpu.CompilerParams(vmem_limit_bytes=4 << 20),
        name="memory_rows",
    )(tail)


def swap(x, axis):
    return lax.all_to_all(x, axis, split_axis=0, concat_axis=0, tiled=True)


def shards(queries, out_grad, mem_keys, mem_values):
    ndoc = lax.axis_size("doc")
    nctx = lax.axis_size("ctx")
    mem = mem_keys.shape[1]
    nchunks = len(CHUNKS)
    blocks = list(by_head(queries[0], out_grad[0], mem_keys[0], mem_values[0], CHUNKS))
    for i in range(nchunks):
        blocks[i] = swap(blocks[i], "ctx")
    memory = swap(memory_copies(blocks[0], CHUNKS[0], mem, ndoc), "doc")
    sums = None
    powers = []
    grads = []
    for i, (block, part) in enumerate(zip(blocks, CHUNKS)):
        grad_q, power, sums = attention_grads(block, part, memory, sums, i == nchunks - 1)
        powers.append(power)
        grads.append(grad_q.reshape(nctx, part, HD))
    sums = swap(sums.astype(HALF), "doc").astype(F32)
    grads[-1] = jnp.concatenate([grads[-1], memory_sums(sums, powers, nctx)], axis=1)
    for i in range(nchunks):
        grads[i] = swap(grads[i].astype(HALF), "ctx")
    tail = grads[-1][:, CHUNKS[-1]:, :].astype(F32)
    grad_k, grad_v = memory_rows(tail, mem, 4 * mem + nchunks)
    grad_q = []
    for i, part in enumerate(CHUNKS):
        scale = jnp.exp2(tail[:, 4 * mem + i, :])[:, None, :]
        grad_q.append(jnp.transpose(grads[i][:, :part, :].astype(F32) * scale, (1, 0, 2)).reshape(part, -1))
    return jnp.concatenate(grad_q, axis=0)[None], grad_k[None], grad_v[None]


def solution(mesh):
    placed = P("doc", "ctx", None)
    return jax.shard_map(
        shards,
        mesh=mesh,
        in_specs=(placed,) * 4,
        out_specs=(placed,) * 3,
        check_vma=False,
    )
```

```python
import jax
import jax.numpy as jnp
from jax import lax
from jax.experimental import pallas as pl
from jax.experimental.pallas import tpu as pltpu
from jax.sharding import PartitionSpec as P


HD = 128
SCALE = HD ** (-0.5)
CHUNKS = (32, 96)
QBLOCK = 512
TILE = 8
HALF_BITS = 14.0
F32 = jnp.float32
BF16 = jnp.bfloat16
HALF = jnp.float16


def dot(a, b, da, db):
    return lax.dot_general(a, b, (((da,), (db,)), ((), ())), preferred_element_type=F32)


def split(x):
    hi = x.astype(BF16)
    return hi, (x - hi.astype(F32)).astype(BF16)


def exponent(top):
    return jnp.ceil(jnp.log2(jnp.maximum(top, 1e-30))) - HALF_BITS


def by_head(queries, out_grad, memory, chunks):
    rows, width = queries.shape
    mem = memory[0].shape[0]
    nheads = width // HD
    group = min(nheads, 8)

    def kernel(q_ref, g_ref, *refs):
        held = [ref[...].astype(F32) for ref in refs[:4]]
        outs = refs[4:]
        for h in range(group):
            cols = slice(h * HD, (h + 1) * HD)
            start = 0
            for out, part in zip(outs, chunks):
                out[h, :part, :] = q_ref[start:start + part, cols]
                out[h, part:2 * part, :] = g_ref[start:start + part, cols]
                start += part
            outs[0][h, 2 * chunks[0]:, :] = jnp.concatenate([x[:, cols] for x in held], axis=0).astype(BF16)

    sizes = [2 * part + (4 * mem if c == 0 else 0) for c, part in enumerate(chunks)]
    return pl.pallas_call(
        kernel,
        grid=(nheads // group,),
        in_specs=[pl.BlockSpec((rows, group * HD), lambda i: (0, i))] * 2
        + [pl.BlockSpec((mem, group * HD), lambda i: (0, i))] * 4,
        out_specs=[pl.BlockSpec((group, size, HD), lambda i: (i, 0, 0)) for size in sizes],
        out_shape=[jax.ShapeDtypeStruct((nheads, size, HD), BF16) for size in sizes],
        cost_estimate=pl.CostEstimate(flops=0, bytes_accessed=8 * rows * width, transcendentals=0),
        name="by_head",
    )(queries, out_grad, *memory)


def held_memory(block, part, rows):
    ndev = block.shape[0]
    total = ndev * rows

    def kernel(x_ref, out, tmp):
        x = x_ref[...].astype(F32)
        for c in range(ndev):
            for t in range(4):
                tmp[t * total + c * rows:t * total + (c + 1) * rows, :] = x[c, t * rows:(t + 1) * rows, :]
        out[0] = tmp[:2 * total, :].astype(BF16)
        out[1] = tmp[2 * total:, :].astype(BF16)

    return pl.pallas_call(
        kernel,
        grid=(1,),
        in_specs=[pl.BlockSpec((ndev, 4 * rows, HD), lambda i: (0, 2 * part // (4 * rows), 0))],
        out_specs=pl.BlockSpec((2, 2 * total, HD), lambda i: (0, 0, 0)),
        out_shape=jax.ShapeDtypeStruct((2, 2 * total, HD), BF16),
        scratch_shapes=[pltpu.VMEM((4 * total, HD), F32)],
        cost_estimate=pl.CostEstimate(flops=0, bytes_accessed=16 * total * HD, transcendentals=0),
        compiler_params=pltpu.CompilerParams(vmem_limit_bytes=4 << 20),
        name="held_memory",
    )(block)


def flip(x, bit, ndoc):
    return lax.ppermute(x, "doc", [(d, d ^ bit) for d in range(ndoc)])


def gather_memory(held, ndoc):
    places = [0, ndoc // 2]
    bit = ndoc // 4
    while True:
        other = flip(held, bit, ndoc)
        places = places + [p ^ bit for p in places]
        if bit == 1:
            return held, other, places
        held = jnp.concatenate([held, other], axis=0)
        bit //= 2


def attention_grads(rows, part, doc, memory, before, last):
    ndev = rows.shape[0]
    held, other, places = memory
    half, both_mem, _ = held.shape
    ndoc = 2 * half
    mem = both_mem // 2
    total = ndoc * mem
    per = max(1, min(ndev, QBLOCK // part))
    while ndev % per:
        per -= 1
    block = per * part
    steps = ndev // per
    size = both_mem + (TILE if last else 0)

    def kernel(*refs):
        if before is None:
            d_ref, x_ref, m0_ref, m1_ref, gq_ref, power_ref, sums_ref, k_ref, v_ref, top_ref = refs
        else:
            d_ref, x_ref, m0_ref, m1_ref, before_ref, gq_ref, power_ref, sums_ref, k_ref, v_ref, top_ref = refs
        acc_ref = sums_ref.at[:, :both_mem, :]
        step = pl.program_id(0)

        @pl.when(step == 0)
        def _():
            acc_ref[...] = jnp.zeros_like(acc_ref) if before is None else before_ref[...]
            for r in range(ndoc):
                m_ref = m0_ref if r < half else m1_ref
                here = pl.ds(pl.multiple_of((d_ref[0] ^ places[r]) * mem, mem), mem)
                k_ref[here, :] = m_ref[r % half, :mem, :]
                v_ref[here, :] = m_ref[r % half, mem:, :]
            top_ref[...] = jnp.zeros_like(top_ref)

        q = x_ref[:, :part, :].reshape(block, HD)
        g = x_ref[:, part:2 * part, :].reshape(block, HD)
        k = k_ref[...]
        v = v_ref[...]
        expo = jnp.exp(dot(k, q, 1, 1) * SCALE)
        dprob = dot(v, g, 1, 1)
        norm = jnp.sum(expo, axis=0, keepdims=True)
        drift = jnp.sum(expo * dprob, axis=0, keepdims=True) / norm
        prob = expo * (1.0 / norm)
        dscore = prob * (dprob - drift)
        p_hi, p_lo = split(prob)
        s_hi, s_lo = split(dscore)
        grad_v = dot(p_hi, g, 1, 0) + dot(p_lo, g, 1, 0)
        grad_k = (dot(s_hi, q, 1, 0) + dot(s_lo, q, 1, 0)) * SCALE
        grad_q = (dot(s_hi, k, 0, 0) + dot(s_lo, k, 0, 0)) * SCALE
        gq_ref[pl.ds(pl.multiple_of(step * block, block), block), :] = grad_q
        top_ref[...] = jnp.maximum(top_ref[...], jnp.max(jnp.abs(grad_q), axis=0, keepdims=True))
        acc_ref[:, :mem, :] += grad_k.reshape(ndoc, mem, HD)
        acc_ref[:, mem:, :] += grad_v.reshape(ndoc, mem, HD)

        @pl.when(step == steps - 1)
        def _():
            power = exponent(jnp.max(top_ref[...], axis=1, keepdims=True))
            gq_ref[...] = gq_ref[...] * jnp.exp2(-power)
            power_ref[...] = jnp.broadcast_to(power, power_ref.shape)
            if last:
                first = lax.broadcasted_iota(jnp.int32, (TILE, HD), 0) == 0
                powers = []
                for start in (0, mem):
                    x = acc_ref[:, start:start + mem, :]
                    top = jnp.max(jnp.max(jnp.max(jnp.abs(x), axis=0), axis=0, keepdims=True), axis=1, keepdims=True)
                    power = exponent(top)
                    acc_ref[:, start:start + mem, :] = x * jnp.exp2(-power).reshape(1, 1, 1)
                    powers.append(jnp.broadcast_to(power, (TILE, HD)))
                tail = jnp.where(first, powers[0], powers[1])
                for d in range(ndoc):
                    sums_ref[d, both_mem:, :] = tail

    def whole(*shape):
        return pl.BlockSpec(shape, lambda i: (0,) * len(shape))

    args = (doc, rows, held, other) if before is None else (doc, rows, held, other, before)
    return pl.pallas_call(
        kernel,
        grid=(steps,),
        in_specs=[
            pl.BlockSpec(memory_space=pltpu.SMEM),
            pl.BlockSpec((per, 2 * part, HD), lambda i: (i, 0, 0)),
            whole(half, both_mem, HD),
            whole(half, both_mem, HD),
        ]
        + [whole(ndoc, both_mem, HD)] * (len(args) - 4),
        out_specs=[whole(ndev * part, HD), whole(1, HD), whole(ndoc, size, HD)],
        out_shape=[
            jax.ShapeDtypeStruct((ndev * part, HD), F32),
            jax.ShapeDtypeStruct((1, HD), F32),
            jax.ShapeDtypeStruct((ndoc, size, HD), F32),
        ],
        scratch_shapes=[pltpu.VMEM((total, HD), BF16)] * 2 + [pltpu.VMEM((1, HD), F32)],
        cost_estimate=pl.CostEstimate(
            flops=16 * ndev * part * total * HD,
            bytes_accessed=8 * ndev * part * HD,
            transcendentals=ndev * part * total,
        ),
        compiler_params=pltpu.CompilerParams(vmem_limit_bytes=24 << 20),
        name="attention_grads",
    )(*args)


def memory_sums(parts, powers, ndev):
    ndoc = parts.shape[0]
    mem = (parts.shape[1] - TILE) // 2
    rows = mem // ndev

    def kernel(x_ref, *refs):
        out = refs[-1]
        terms = []
        last = [p[...] for p in refs[:-1]]
        for v in (0, 1):
            total = jnp.zeros((mem, HD), F32)
            for d in range(ndoc):
                total = total + x_ref[d, v * mem:(v + 1) * mem, :] * jnp.exp2(x_ref[d, 2 * mem + v:2 * mem + v + 1, :])
            top = jnp.max(jnp.max(jnp.abs(total), axis=0, keepdims=True), axis=1, keepdims=True)
            power = exponent(top)
            total = total * jnp.exp2(-power)
            high = total.astype(BF16).astype(F32)
            terms += [high, total - high]
            last.append(jnp.broadcast_to(power, (1, HD)))
        last = jnp.concatenate(last + [jnp.zeros((2 * TILE - 4 * rows - len(last), HD), F32)], axis=0)
        for c in range(ndev):
            for t, term in enumerate(terms):
                out[c, t * rows:(t + 1) * rows, :] = term[c * rows:(c + 1) * rows, :]
            out[c, 4 * rows:, :] = last

    return pl.pallas_call(
        kernel,
        out_shape=jax.ShapeDtypeStruct((ndev, 2 * TILE, HD), F32),
        cost_estimate=pl.CostEstimate(flops=0, bytes_accessed=4 * parts.size, transcendentals=0),
        compiler_params=pltpu.CompilerParams(vmem_limit_bytes=6 << 20),
        name="memory_sums",
    )(parts, *powers)


def memory_rows(tail, rows, at):
    nheads = tail.shape[0]

    def kernel(x_ref, k_ref, v_ref):
        for h in range(nheads):
            cols = slice(h * HD, (h + 1) * HD)
            scale = jnp.exp2(x_ref[h, at:at + 2, :])
            k_ref[:, cols] = (x_ref[h, :rows, :] + x_ref[h, rows:2 * rows, :]) * scale[:1]
            v_ref[:, cols] = (x_ref[h, 2 * rows:3 * rows, :] + x_ref[h, 3 * rows:4 * rows, :]) * scale[1:]

    return pl.pallas_call(
        kernel,
        out_shape=[jax.ShapeDtypeStruct((rows, nheads * HD), F32)] * 2,
        cost_estimate=pl.CostEstimate(flops=0, bytes_accessed=16 * nheads * TILE * HD, transcendentals=0),
        compiler_params=pltpu.CompilerParams(vmem_limit_bytes=4 << 20),
        name="memory_rows",
    )(tail)


def swap(x, axis):
    return lax.all_to_all(x, axis, split_axis=0, concat_axis=0, tiled=True)


def shards(queries, out_grad, mem_keys, mem_values):
    ndoc = lax.axis_size("doc")
    nctx = lax.axis_size("ctx")
    mem = mem_keys.shape[1]
    nchunks = len(CHUNKS)
    doc = lax.axis_index("doc").reshape(1)
    memory = [mem_keys[0], mem_values[0]]
    memory = memory + [flip(x, ndoc // 2, ndoc) for x in memory]
    blocks = list(by_head(queries[0], out_grad[0], memory, CHUNKS))
    for i in range(nchunks):
        blocks[i] = swap(blocks[i], "ctx")
    memory = gather_memory(held_memory(blocks[0], CHUNKS[0], mem), ndoc)
    sums = None
    powers = []
    grads = []
    for i, (block, part) in enumerate(zip(blocks, CHUNKS)):
        grad_q, power, sums = attention_grads(block, part, doc, memory, sums, i == nchunks - 1)
        powers.append(power)
        grads.append(grad_q.reshape(nctx, part, HD))
    sums = swap(sums.astype(HALF), "doc").astype(F32)
    grads[-1] = jnp.concatenate([grads[-1], memory_sums(sums, powers, nctx)], axis=1)
    for i in range(nchunks):
        grads[i] = swap(grads[i].astype(HALF), "ctx")
    tail = grads[-1][:, CHUNKS[-1]:, :].astype(F32)
    grad_k, grad_v = memory_rows(tail, mem, 4 * mem + nchunks)
    grad_q = []
    for i, part in enumerate(CHUNKS):
        scale = jnp.exp2(tail[:, 4 * mem + i, :])[:, None, :]
        grad_q.append(jnp.transpose(grads[i][:, :part, :].astype(F32) * scale, (1, 0, 2)).reshape(part, -1))
    return jnp.concatenate(grad_q, axis=0)[None], grad_k[None], grad_v[None]


def solution(mesh):
    placed = P("doc", "ctx", None)
    return jax.shard_map(
        shards,
        mesh=mesh,
        in_specs=(placed,) * 4,
        out_specs=(placed,) * 3,
        check_vma=False,
    )
```

```python
import jax
import jax.numpy as jnp
from jax import lax
from jax.experimental import pallas as pl
from jax.experimental.pallas import tpu as pltpu
from jax.sharding import PartitionSpec as P


HD = 128
SCALE = HD ** (-0.5)
CHUNKS = (48, 80)
QBLOCK = 640
TILE = 8
HALF_BITS = 14.0
F32 = jnp.float32
BF16 = jnp.bfloat16
HALF = jnp.float16


def dot(a, b, da, db):
    return lax.dot_general(a, b, (((da,), (db,)), ((), ())), preferred_element_type=F32)


def split(x):
    hi = x.astype(BF16)
    return hi, (x - hi.astype(F32)).astype(BF16)


def exponent(top):
    return jnp.ceil(jnp.log2(jnp.maximum(top, 1e-30))) - HALF_BITS


def by_head(queries, out_grad, memory, chunks):
    rows, width = queries.shape
    mem = memory[0].shape[0]
    nheads = width // HD
    group = min(nheads, 8)

    def kernel(q_ref, g_ref, *refs):
        held = [ref[...].astype(F32) for ref in refs[:2]]
        held.append(jnp.zeros((TILE - 2 * mem, held[0].shape[1]), F32))
        outs = refs[2:]
        for h in range(group):
            cols = slice(h * HD, (h + 1) * HD)
            start = 0
            for out, part in zip(outs, chunks):
                out[h, :part, :] = q_ref[start:start + part, cols]
                out[h, part:2 * part, :] = g_ref[start:start + part, cols]
                start += part
            outs[0][h, 2 * chunks[0]:, :] = jnp.concatenate([x[:, cols] for x in held], axis=0).astype(BF16)

    sizes = [2 * part + (TILE if c == 0 else 0) for c, part in enumerate(chunks)]
    return pl.pallas_call(
        kernel,
        grid=(nheads // group,),
        in_specs=[pl.BlockSpec((rows, group * HD), lambda i: (0, i))] * 2
        + [pl.BlockSpec((mem, group * HD), lambda i: (0, i))] * 2,
        out_specs=[pl.BlockSpec((group, size, HD), lambda i: (i, 0, 0)) for size in sizes],
        out_shape=[jax.ShapeDtypeStruct((nheads, size, HD), BF16) for size in sizes],
        cost_estimate=pl.CostEstimate(flops=0, bytes_accessed=8 * rows * width, transcendentals=0),
        name="by_head",
    )(queries, out_grad, *memory)


def own_memory(block, part, rows):
    ndev = block.shape[0]
    total = ndev * rows

    def kernel(x_ref, out, tmp):
        x = x_ref[...].astype(F32)
        for c in range(ndev):
            tmp[c * rows:(c + 1) * rows, :] = x[c, :rows, :]
            tmp[total + c * rows:total + (c + 1) * rows, :] = x[c, rows:2 * rows, :]
        out[0] = tmp[...].astype(BF16)

    return pl.pallas_call(
        kernel,
        grid=(1,),
        in_specs=[pl.BlockSpec((ndev, TILE, HD), lambda i: (0, 2 * part // TILE, 0))],
        out_specs=pl.BlockSpec((1, 2 * total, HD), lambda i: (0, 0, 0)),
        out_shape=jax.ShapeDtypeStruct((1, 2 * total, HD), BF16),
        scratch_shapes=[pltpu.VMEM((2 * total, HD), F32)],
        cost_estimate=pl.CostEstimate(flops=0, bytes_accessed=8 * total * HD, transcendentals=0),
        compiler_params=pltpu.CompilerParams(vmem_limit_bytes=4 << 20),
        name="own_memory",
    )(block)


def gather_memory(held, ndoc):
    places = [0]
    bit = ndoc // 2
    while True:
        other = lax.ppermute(held, "doc", [(d, d ^ bit) for d in range(ndoc)])
        places = places + [p ^ bit for p in places]
        if bit == 1:
            return held, other, places
        held = jnp.concatenate([held, other], axis=0)
        bit //= 2


def attention_grads(rows, part, doc, memory, before, last):
    ndev = rows.shape[0]
    held, other, places = memory
    half, both_mem, _ = held.shape
    ndoc = 2 * half
    mem = both_mem // 2
    total = ndoc * mem
    per = max(1, min(ndev, QBLOCK // part))
    while ndev % per:
        per -= 1
    block = per * part
    steps = ndev // per
    size = both_mem + (TILE if last else 0)

    def kernel(*refs):
        if before is None:
            d_ref, x_ref, m0_ref, m1_ref, gq_ref, power_ref, sums_ref, k_ref, v_ref, kt_ref, top_ref = refs
        else:
            d_ref, x_ref, m0_ref, m1_ref, before_ref, gq_ref, power_ref, sums_ref, k_ref, v_ref, kt_ref, top_ref = refs
        acc_ref = sums_ref.at[:, :both_mem, :]
        step = pl.program_id(0)

        @pl.when(step == 0)
        def _():
            acc_ref[...] = jnp.zeros_like(acc_ref) if before is None else before_ref[...]
            for r in range(ndoc):
                m_ref = m0_ref if r < half else m1_ref
                here = pl.ds(pl.multiple_of((d_ref[0] ^ places[r]) * mem, mem), mem)
                k_ref[here, :] = m_ref[r % half, :mem, :]
                v_ref[here, :] = m_ref[r % half, mem:, :]
            kt_ref[...] = jnp.transpose(k_ref[...].astype(F32)).astype(BF16)
            top_ref[...] = jnp.zeros_like(top_ref)

        q = x_ref[:, :part, :].reshape(block, HD)
        g = x_ref[:, part:2 * part, :].reshape(block, HD)
        k = k_ref[...]
        v = v_ref[...]
        expo = jnp.exp(dot(k, q, 1, 1) * SCALE)
        dprob = dot(v, g, 1, 1)
        norm = jnp.sum(expo, axis=0, keepdims=True)
        drift = jnp.sum(expo * dprob, axis=0, keepdims=True) / norm
        prob = expo * (1.0 / norm)
        dscore = prob * (dprob - drift)
        p_hi, p_lo = split(prob)
        s_hi, s_lo = split(dscore)
        grad_v = dot(p_hi, g, 1, 0) + dot(p_lo, g, 1, 0)
        grad_k = (dot(s_hi, q, 1, 0) + dot(s_lo, q, 1, 0)) * SCALE
        kt = kt_ref[...]
        grad_q = jnp.transpose(dot(kt, s_hi, 1, 0) + dot(kt, s_lo, 1, 0)) * SCALE
        gq_ref[pl.ds(pl.multiple_of(step * block, block), block), :] = grad_q
        top_ref[...] = jnp.maximum(top_ref[...], jnp.max(jnp.abs(grad_q), axis=0, keepdims=True))
        acc_ref[:, :mem, :] += grad_k.reshape(ndoc, mem, HD)
        acc_ref[:, mem:, :] += grad_v.reshape(ndoc, mem, HD)

        @pl.when(step == steps - 1)
        def _():
            power = exponent(jnp.max(top_ref[...], axis=1, keepdims=True))
            gq_ref[...] = gq_ref[...] * jnp.exp2(-power)
            power_ref[...] = jnp.broadcast_to(power, power_ref.shape)
            if last:
                first = lax.broadcasted_iota(jnp.int32, (TILE, HD), 0) == 0
                powers = []
                for start in (0, mem):
                    x = acc_ref[:, start:start + mem, :]
                    top = jnp.max(jnp.max(jnp.max(jnp.abs(x), axis=0), axis=0, keepdims=True), axis=1, keepdims=True)
                    power = exponent(top)
                    acc_ref[:, start:start + mem, :] = x * jnp.exp2(-power).reshape(1, 1, 1)
                    powers.append(jnp.broadcast_to(power, (TILE, HD)))
                tail = jnp.where(first, powers[0], powers[1])
                for d in range(ndoc):
                    sums_ref[d, both_mem:, :] = tail

    def whole(*shape):
        return pl.BlockSpec(shape, lambda i: (0,) * len(shape))

    args = (doc, rows, held, other) if before is None else (doc, rows, held, other, before)
    return pl.pallas_call(
        kernel,
        grid=(steps,),
        in_specs=[
            pl.BlockSpec(memory_space=pltpu.SMEM),
            pl.BlockSpec((per, 2 * part, HD), lambda i: (i, 0, 0)),
            whole(half, both_mem, HD),
            whole(half, both_mem, HD),
        ]
        + [whole(ndoc, both_mem, HD)] * (len(args) - 4),
        out_specs=[whole(ndev * part, HD), whole(1, HD), whole(ndoc, size, HD)],
        out_shape=[
            jax.ShapeDtypeStruct((ndev * part, HD), F32),
            jax.ShapeDtypeStruct((1, HD), F32),
            jax.ShapeDtypeStruct((ndoc, size, HD), F32),
        ],
        scratch_shapes=[
            pltpu.VMEM((total, HD), BF16),
            pltpu.VMEM((total, HD), BF16),
            pltpu.VMEM((HD, total), BF16),
            pltpu.VMEM((1, HD), F32),
        ],
        cost_estimate=pl.CostEstimate(
            flops=16 * ndev * part * total * HD,
            bytes_accessed=8 * ndev * part * HD,
            transcendentals=ndev * part * total,
        ),
        compiler_params=pltpu.CompilerParams(vmem_limit_bytes=24 << 20),
        name="attention_grads",
    )(*args)


def memory_sums(parts, powers, ndev):
    ndoc = parts.shape[0]
    mem = (parts.shape[1] - TILE) // 2
    rows = mem // ndev

    def kernel(x_ref, *refs):
        out = refs[-1]
        terms = []
        last = [p[...] for p in refs[:-1]]
        for v in (0, 1):
            total = jnp.zeros((mem, HD), F32)
            for d in range(ndoc):
                total = total + x_ref[d, v * mem:(v + 1) * mem, :] * jnp.exp2(x_ref[d, 2 * mem + v:2 * mem + v + 1, :])
            top = jnp.max(jnp.max(jnp.abs(total), axis=0, keepdims=True), axis=1, keepdims=True)
            power = exponent(top)
            total = total * jnp.exp2(-power)
            high = total.astype(BF16).astype(F32)
            terms += [high, total - high]
            last.append(jnp.broadcast_to(power, (1, HD)))
        last = jnp.concatenate(last + [jnp.zeros((2 * TILE - 4 * rows - len(last), HD), F32)], axis=0)
        for c in range(ndev):
            for t, term in enumerate(terms):
                out[c, t * rows:(t + 1) * rows, :] = term[c * rows:(c + 1) * rows, :]
            out[c, 4 * rows:, :] = last

    return pl.pallas_call(
        kernel,
        out_shape=jax.ShapeDtypeStruct((ndev, 2 * TILE, HD), F32),
        cost_estimate=pl.CostEstimate(flops=0, bytes_accessed=4 * parts.size, transcendentals=0),
        compiler_params=pltpu.CompilerParams(vmem_limit_bytes=6 << 20),
        name="memory_sums",
    )(parts, *powers)


def memory_rows(tail, rows, at):
    nheads = tail.shape[0]

    def kernel(x_ref, k_ref, v_ref):
        for h in range(nheads):
            cols = slice(h * HD, (h + 1) * HD)
            scale = jnp.exp2(x_ref[h, at:at + 2, :])
            k_ref[:, cols] = (x_ref[h, :rows, :] + x_ref[h, rows:2 * rows, :]) * scale[:1]
            v_ref[:, cols] = (x_ref[h, 2 * rows:3 * rows, :] + x_ref[h, 3 * rows:4 * rows, :]) * scale[1:]

    return pl.pallas_call(
        kernel,
        out_shape=[jax.ShapeDtypeStruct((rows, nheads * HD), F32)] * 2,
        cost_estimate=pl.CostEstimate(flops=0, bytes_accessed=16 * nheads * TILE * HD, transcendentals=0),
        compiler_params=pltpu.CompilerParams(vmem_limit_bytes=4 << 20),
        name="memory_rows",
    )(tail)


def swap(x, axis):
    return lax.all_to_all(x, axis, split_axis=0, concat_axis=0, tiled=True)


def shards(queries, out_grad, mem_keys, mem_values):
    ndoc = lax.axis_size("doc")
    nctx = lax.axis_size("ctx")
    mem = mem_keys.shape[1]
    nchunks = len(CHUNKS)
    doc = lax.axis_index("doc").reshape(1)
    blocks = list(by_head(queries[0], out_grad[0], [mem_keys[0], mem_values[0]], CHUNKS))
    for i in range(nchunks):
        blocks[i] = swap(blocks[i], "ctx")
    memory = gather_memory(own_memory(blocks[0], CHUNKS[0], mem), ndoc)
    sums = None
    powers = []
    grads = []
    for i, (block, part) in enumerate(zip(blocks, CHUNKS)):
        grad_q, power, sums = attention_grads(block, part, doc, memory, sums, i == nchunks - 1)
        powers.append(power)
        grads.append(grad_q.reshape(nctx, part, HD))
    sums = swap(sums.astype(HALF), "doc").astype(F32)
    grads[-1] = jnp.concatenate([grads[-1], memory_sums(sums, powers, nctx)], axis=1)
    for i in range(nchunks):
        grads[i] = swap(grads[i].astype(HALF), "ctx")
    tail = grads[-1][:, CHUNKS[-1]:, :].astype(F32)
    grad_k, grad_v = memory_rows(tail, mem, 4 * mem + nchunks)
    grad_q = []
    for i, part in enumerate(CHUNKS):
        scale = jnp.exp2(tail[:, 4 * mem + i, :])[:, None, :]
        grad_q.append(jnp.transpose(grads[i][:, :part, :].astype(F32) * scale, (1, 0, 2)).reshape(part, -1))
    return jnp.concatenate(grad_q, axis=0)[None], grad_k[None], grad_v[None]


def solution(mesh):
    placed = P("doc", "ctx", None)
    return jax.shard_map(
        shards,
        mesh=mesh,
        in_specs=(placed,) * 4,
        out_specs=(placed,) * 3,
        check_vma=False,
    )
```

```python
import math

import jax
import jax.numpy as jnp
from jax import lax
from jax.experimental import pallas as pl
from jax.experimental.pallas import tpu as pltpu
from jax.sharding import PartitionSpec as P


HD = 128
SCALE = HD ** (-0.5)
CHUNKS = (64, 64)
QBLOCK = 512
TILE = 8
HALF_BITS = 14.0
F32 = jnp.float32
BF16 = jnp.bfloat16
HALF = jnp.float16


def dot(a, b, da, db):
    return lax.dot_general(a, b, (((da,), (db,)), ((), ())), preferred_element_type=F32)


def split(x):
    hi = x.astype(BF16)
    return hi, (x - hi.astype(F32)).astype(BF16)


def exponent(top):
    return jnp.ceil(jnp.log2(jnp.maximum(top, 1e-30))) - HALF_BITS


def by_head(queries, out_grad, start, part, memory=()):
    _, width = queries.shape
    nheads = width // HD
    group = min(nheads, 8)
    step = math.gcd(start, part) or part
    size = 2 * part + (TILE if memory else 0)
    blocks = part // step

    def kernel(*refs):
        out = refs[-1]
        q_refs, g_refs, m_refs = refs[:blocks], refs[blocks:2 * blocks], refs[2 * blocks:-1]
        held = [ref[...].astype(F32) for ref in m_refs]
        if held:
            held.append(jnp.zeros((TILE - sum(x.shape[0] for x in held), group * HD), F32))
        for h in range(group):
            cols = slice(h * HD, (h + 1) * HD)
            for b in range(blocks):
                out[h, b * step:(b + 1) * step, :] = q_refs[b][:, cols]
                out[h, part + b * step:part + (b + 1) * step, :] = g_refs[b][:, cols]
            if held:
                out[h, 2 * part:, :] = jnp.concatenate([x[:, cols] for x in held], axis=0).astype(BF16)

    token_specs = [pl.BlockSpec((step, group * HD), lambda i, b=b: (start // step + b, i)) for b in range(blocks)]
    return pl.pallas_call(
        kernel,
        grid=(nheads // group,),
        in_specs=token_specs * 2 + [pl.BlockSpec((x.shape[0], group * HD), lambda i: (0, i)) for x in memory],
        out_specs=pl.BlockSpec((group, size, HD), lambda i: (i, 0, 0)),
        out_shape=jax.ShapeDtypeStruct((nheads, size, HD), BF16),
        cost_estimate=pl.CostEstimate(flops=0, bytes_accessed=8 * part * width, transcendentals=0),
        name="by_head",
    )(*[queries] * blocks, *[out_grad] * blocks, *memory)


def memory_copies(block, part, rows, ndoc):
    ndev = block.shape[0]
    total = ndev * rows

    def kernel(x_ref, out, tmp):
        x = x_ref[...].astype(F32)
        for c in range(ndev):
            tmp[c * rows:(c + 1) * rows, :] = x[c, :rows, :]
            tmp[total + c * rows:total + (c + 1) * rows, :] = x[c, rows:2 * rows, :]
        whole = tmp[...].astype(BF16)
        for d in range(ndoc):
            out[d] = whole

    return pl.pallas_call(
        kernel,
        grid=(1,),
        in_specs=[pl.BlockSpec((ndev, TILE, HD), lambda i: (0, 2 * part // TILE, 0))],
        out_specs=pl.BlockSpec((ndoc, 2 * total, HD), lambda i: (0, 0, 0)),
        out_shape=jax.ShapeDtypeStruct((ndoc, 2 * total, HD), BF16),
        scratch_shapes=[pltpu.VMEM((2 * total, HD), F32)],
        cost_estimate=pl.CostEstimate(flops=0, bytes_accessed=4 * ndoc * total * HD, transcendentals=0),
        compiler_params=pltpu.CompilerParams(vmem_limit_bytes=4 << 20),
        name="memory_copies",
    )(block)


def attention_grads(rows, part, memory, before, last):
    ndev = rows.shape[0]
    ndoc, both_mem, _ = memory.shape
    mem = both_mem // 2
    total = ndoc * mem
    per = max(1, min(ndev, QBLOCK // part))
    while ndev % per:
        per -= 1
    block = per * part
    steps = ndev // per
    size = both_mem + (TILE if last else 0)

    def kernel(*refs):
        if before is None:
            x_ref, m_ref, gq_ref, power_ref, sums_ref, k_ref, v_ref, kt_ref, top_ref = refs
        else:
            x_ref, m_ref, before_ref, gq_ref, power_ref, sums_ref, k_ref, v_ref, kt_ref, top_ref = refs
        acc_ref = sums_ref.at[:, :both_mem, :]
        step = pl.program_id(0)

        @pl.when(step == 0)
        def _():
            acc_ref[...] = jnp.zeros_like(acc_ref) if before is None else before_ref[...]
            k_ref[...] = m_ref[:, :mem, :].reshape(total, HD)
            v_ref[...] = m_ref[:, mem:, :].reshape(total, HD)
            kt_ref[...] = jnp.transpose(k_ref[...].astype(F32)).astype(BF16)
            top_ref[...] = jnp.zeros_like(top_ref)

        q = x_ref[:, :part, :].reshape(block, HD)
        g = x_ref[:, part:2 * part, :].reshape(block, HD)
        k = k_ref[...]
        v = v_ref[...]
        expo = jnp.exp(dot(k, q, 1, 1) * SCALE)
        dprob = dot(v, g, 1, 1)
        norm = jnp.sum(expo, axis=0, keepdims=True)
        drift = jnp.sum(expo * dprob, axis=0, keepdims=True) / norm
        prob = expo * (1.0 / norm)
        dscore = prob * (dprob - drift)
        p_hi, p_lo = split(prob)
        s_hi, s_lo = split(dscore)
        grad_v = dot(p_hi, g, 1, 0) + dot(p_lo, g, 1, 0)
        grad_k = (dot(s_hi, q, 1, 0) + dot(s_lo, q, 1, 0)) * SCALE
        kt = kt_ref[...]
        grad_q = jnp.transpose(dot(kt, s_hi, 1, 0) + dot(kt, s_lo, 1, 0)) * SCALE
        gq_ref[pl.ds(pl.multiple_of(step * block, block), block), :] = grad_q
        top_ref[...] = jnp.maximum(top_ref[...], jnp.max(jnp.abs(grad_q), axis=0, keepdims=True))
        acc_ref[:, :mem, :] += grad_k.reshape(ndoc, mem, HD)
        acc_ref[:, mem:, :] += grad_v.reshape(ndoc, mem, HD)

        @pl.when(step == steps - 1)
        def _():
            power = exponent(jnp.max(top_ref[...], axis=1, keepdims=True))
            gq_ref[...] = gq_ref[...] * jnp.exp2(-power)
            power_ref[...] = jnp.broadcast_to(power, power_ref.shape)
            if last:
                first = lax.broadcasted_iota(jnp.int32, (TILE, HD), 0) == 0
                powers = []
                for start in (0, mem):
                    x = acc_ref[:, start:start + mem, :]
                    top = jnp.max(jnp.max(jnp.max(jnp.abs(x), axis=0), axis=0, keepdims=True), axis=1, keepdims=True)
                    power = exponent(top)
                    acc_ref[:, start:start + mem, :] = x * jnp.exp2(-power).reshape(1, 1, 1)
                    powers.append(jnp.broadcast_to(power, (TILE, HD)))
                tail = jnp.where(first, powers[0], powers[1])
                for d in range(ndoc):
                    sums_ref[d, both_mem:, :] = tail

    def whole(*shape):
        return pl.BlockSpec(shape, lambda i: (0,) * len(shape))

    args = (rows, memory) if before is None else (rows, memory, before)
    return pl.pallas_call(
        kernel,
        grid=(steps,),
        in_specs=[pl.BlockSpec((per, 2 * part, HD), lambda i: (i, 0, 0))]
        + [whole(ndoc, both_mem, HD)] * (len(args) - 1),
        out_specs=[whole(ndev * part, HD), whole(1, HD), whole(ndoc, size, HD)],
        out_shape=[
            jax.ShapeDtypeStruct((ndev * part, HD), F32),
            jax.ShapeDtypeStruct((1, HD), F32),
            jax.ShapeDtypeStruct((ndoc, size, HD), F32),
        ],
        scratch_shapes=[
            pltpu.VMEM((total, HD), BF16),
            pltpu.VMEM((total, HD), BF16),
            pltpu.VMEM((HD, total), BF16),
            pltpu.VMEM((1, HD), F32),
        ],
        cost_estimate=pl.CostEstimate(
            flops=16 * ndev * part * total * HD,
            bytes_accessed=8 * ndev * part * HD,
            transcendentals=ndev * part * total,
        ),
        compiler_params=pltpu.CompilerParams(vmem_limit_bytes=24 << 20),
        name="attention_grads",
    )(*args)


def memory_sums(parts, powers, ndev):
    ndoc = parts.shape[0]
    mem = (parts.shape[1] - TILE) // 2
    rows = mem // ndev

    def kernel(x_ref, *refs):
        out = refs[-1]
        terms = []
        last = [p[...] for p in refs[:-1]]
        for v in (0, 1):
            total = jnp.zeros((mem, HD), F32)
            for d in range(ndoc):
                total = total + x_ref[d, v * mem:(v + 1) * mem, :] * jnp.exp2(x_ref[d, 2 * mem + v:2 * mem + v + 1, :])
            top = jnp.max(jnp.max(jnp.abs(total), axis=0, keepdims=True), axis=1, keepdims=True)
            power = exponent(top)
            total = total * jnp.exp2(-power)
            high = total.astype(BF16).astype(F32)
            terms += [high, total - high]
            last.append(jnp.broadcast_to(power, (1, HD)))
        last = jnp.concatenate(last + [jnp.zeros((2 * TILE - 4 * rows - len(last), HD), F32)], axis=0)
        for c in range(ndev):
            for t, term in enumerate(terms):
                out[c, t * rows:(t + 1) * rows, :] = term[c * rows:(c + 1) * rows, :]
            out[c, 4 * rows:, :] = last

    return pl.pallas_call(
        kernel,
        out_shape=jax.ShapeDtypeStruct((ndev, 2 * TILE, HD), F32),
        cost_estimate=pl.CostEstimate(flops=0, bytes_accessed=4 * parts.size, transcendentals=0),
        compiler_params=pltpu.CompilerParams(vmem_limit_bytes=6 << 20),
        name="memory_sums",
    )(parts, *powers)


def memory_rows(tail, rows, at):
    nheads = tail.shape[0]

    def kernel(x_ref, k_ref, v_ref):
        for h in range(nheads):
            cols = slice(h * HD, (h + 1) * HD)
            scale = jnp.exp2(x_ref[h, at:at + 2, :])
            k_ref[:, cols] = (x_ref[h, :rows, :] + x_ref[h, rows:2 * rows, :]) * scale[:1]
            v_ref[:, cols] = (x_ref[h, 2 * rows:3 * rows, :] + x_ref[h, 3 * rows:4 * rows, :]) * scale[1:]

    return pl.pallas_call(
        kernel,
        out_shape=[jax.ShapeDtypeStruct((rows, nheads * HD), F32)] * 2,
        cost_estimate=pl.CostEstimate(flops=0, bytes_accessed=16 * nheads * TILE * HD, transcendentals=0),
        compiler_params=pltpu.CompilerParams(vmem_limit_bytes=4 << 20),
        name="memory_rows",
    )(tail)


def swap(x, axis):
    return lax.all_to_all(x, axis, split_axis=0, concat_axis=0, tiled=True)


def shards(queries, out_grad, mem_keys, mem_values):
    ndoc = lax.axis_size("doc")
    nctx = lax.axis_size("ctx")
    mem = mem_keys.shape[1]
    nchunks = len(CHUNKS)
    blocks = []
    for i, part in enumerate(CHUNKS):
        extra = (mem_keys[0], mem_values[0]) if i == 0 else ()
        block = by_head(queries[0], out_grad[0], sum(CHUNKS[:i]), part, extra)
        blocks.append(swap(block, "ctx"))
    memory = swap(memory_copies(blocks[0], CHUNKS[0], mem, ndoc), "doc")
    sums = None
    powers = []
    grads = []
    for i, (block, part) in enumerate(zip(blocks, CHUNKS)):
        grad_q, power, sums = attention_grads(block, part, memory, sums, i == nchunks - 1)
        powers.append(power)
        grads.append(grad_q.reshape(nctx, part, HD))
    sums = swap(sums.astype(HALF), "doc").astype(F32)
    grads[-1] = jnp.concatenate([grads[-1], memory_sums(sums, powers, nctx)], axis=1)
    for i in range(nchunks):
        grads[i] = swap(grads[i].astype(HALF), "ctx")
    tail = grads[-1][:, CHUNKS[-1]:, :].astype(F32)
    grad_k, grad_v = memory_rows(tail, mem, 4 * mem + nchunks)
    grad_q = []
    for i, part in enumerate(CHUNKS):
        scale = jnp.exp2(tail[:, 4 * mem + i, :])[:, None, :]
        grad_q.append(jnp.transpose(grads[i][:, :part, :].astype(F32) * scale, (1, 0, 2)).reshape(part, -1))
    return jnp.concatenate(grad_q, axis=0)[None], grad_k[None], grad_v[None]


def solution(mesh):
    placed = P("doc", "ctx", None)
    return jax.shard_map(
        shards,
        mesh=mesh,
        in_specs=(placed,) * 4,
        out_specs=(placed,) * 3,
        check_vma=False,
    )
```
